32 devices in a mesh: groups: 2 (over x), col: 16 (over z, y, core).
Axes of the slice: x: 2, y: 2, z: 4, core: 2. Of those that a mesh axis runs over, the one named last changes fastest.
Arguments:
- queries: bfloat16 [4096, 896], P(('groups', 'col')), parts along dimension 0, may hold values from -128 to 128
- keys: bfloat16 [4096, 128], P(('groups', 'col')), parts along dimension 0, may hold values from -6 to 6
- values: bfloat16 [4096, 128], P(('groups', 'col')), parts along dimension 0, may hold values from -6 to 6
- out_weight: bfloat16 [896, 3584], replicated, may hold values from -6 to 6
Outputs:
- projected: bfloat16 [4096, 3584], P(('groups', 'col')), parts along dimension 0
The draws below stay inside these ranges and needn't reach their ends.
There are 2 independent parts, one for each index of `groups`. The reference program is written for one: setup_inputs(seed, part) draws one part's arguments, and reference() takes and returns one part's arrays. A program takes and returns all parts, laid end to end along the dimension named above; an argument that names none is the same for every part. Nothing has to cross between parts.
All inputs are finite; a program needn't handle non-finite values.
Results may differ from the reference program's by a relative error of at most 0.0095.
Values may be sent and summed in bfloat16 or wider, within the bound.
No kernel may reach another device: no remote copies, remote signals or barrier semaphores. Data moves between devices by JAX's collectives and lax.ppermute only.
A program may use at most 64 MiB of HBM per device.

```python
import math
import jax
import jax.numpy as jnp
from jax import lax

D = 3584
HD = 128
QHEADS = 7
TOKENS = 2048


def pair_draw(key):
    base = jax.random.fold_in(key, 11)
    first, second = jax.random.split(base, 2)
    key_rows = jnp.clip(jax.random.normal(first, (TOKENS, HD), jnp.float32), -5.0, 5.0)
    query_rows = jnp.clip(jax.random.normal(second, (TOKENS, QHEADS * HD), jnp.float32), -6.0, 6.0)
    return (query_rows, key_rows)


def draw_queries(key, part):
    return pair_draw(key)[0].astype(jnp.bfloat16)


def draw_keys(key, part):
    return pair_draw(key)[1].astype(jnp.bfloat16)


def block_levels(stream_key, shape, pieces, low, high):
    factor_of = 1.0
    for axis_at, shards_of in pieces:
        heights = jax.random.uniform(jax.random.fold_in(jax.random.fold_in(stream_key, 6), axis_at), (shards_of,), jnp.float32, low / len(pieces), high / len(pieces))
        factor_of = factor_of * jnp.repeat(jnp.exp(heights), shape[axis_at] // shards_of).reshape((-1,) + (1,) * (len(shape) - 1 - axis_at))
    return factor_of


def gaussian(stream_key, dims, scale, reach, pieces=(), held_as=jnp.bfloat16):
    drawn = jax.random.normal(stream_key, dims, jnp.float32) * scale
    if len(pieces) > 0:
        drawn = block_levels(stream_key, dims, pieces, -0.22, 0.18) * drawn
    return jnp.clip(drawn, min=-reach, max=reach).astype(held_as)


def setup_inputs(seed: int = 0, part: int = 0) -> dict:
    arg_keys = jax.random.split(jax.random.key(seed), 5)
    part_splits = jax.random.split(jax.random.fold_in(arg_keys[4], part), 5)
    queries = draw_queries(jax.random.fold_in(jax.random.fold_in(arg_keys[4], part), 71), part)
    keys = draw_keys(jax.random.fold_in(jax.random.fold_in(arg_keys[4], part), 71), part)
    values = gaussian(part_splits[2], (TOKENS, HD), 1.0, 6.0, ((0, 16),))
    out_weight = gaussian(arg_keys[3], (QHEADS * HD, D), ((TOKENS / (3 * QHEADS * HD)) ** 0.5), 6.0)
    return {"queries": queries, "keys": keys, "values": values, "out_weight": out_weight}


def reference(queries, keys, values, out_weight):
    factor = HD ** -0.5
    key_rows = keys.astype(jnp.float32)
    value_rows = values.astype(jnp.float32)
    block = math.gcd(TOKENS, 512)
    query_blocks = queries.reshape(TOKENS // block, block, QHEADS, HD)

    def attend_block(query_block):
        scores = jnp.einsum('thd,sd->hts', query_block.astype(jnp.float32), key_rows) * factor
        highest = jnp.max(scores, axis=-1, keepdims=True)
        expo = jnp.exp(scores - highest)
        total = jnp.sum(expo, axis=-1)
        weights = expo.astype(jnp.bfloat16).astype(jnp.float32)
        numerator = jnp.einsum('hts,sd->thd', weights, value_rows)
        return (numerator / jnp.transpose(total)[:, :, None]).astype(jnp.bfloat16)

    attended = lax.map(attend_block, query_blocks).reshape(TOKENS, QHEADS * HD)
    return jnp.dot(attended, out_weight, preferred_element_type=jnp.float32).astype(jnp.bfloat16)
```

```python
import math

import jax
import jax.numpy as jnp
from jax import lax
from jax.experimental import pallas as pl
from jax.experimental.pallas import tpu as pltpu
from jax.sharding import PartitionSpec as P

LANES = 128
BLOCK = 1024
HOPS = (
    (8, (0,)),
    (4, (0,)),
    (2, (0,)),
    (1, (0,)),
    (4, (8,)),
    (1, (2, 4)),
    (2, (4, 8)),
    (1, (8, 12)),
    (2, (12,)),
    (1, (6, 10)),
    (1, (14,)),
)
GROUPS = ((-1, 3), (0, 1, 2, 4, 5, 7), (6, 9, 8, 10))


def in_vmem(x):
    return pltpu.with_memory_space_constraint(x, pltpu.VMEM)


def softmax_block(query, keys, values, state, scale):
    rows = query.shape[0]
    tiles = keys.shape[0] // LANES
    scores = lax.dot_general(query, keys, (((1,), (1,)), ((), ())), preferred_element_type=jnp.float32)
    parts = [scores[:, i * LANES : (i + 1) * LANES] for i in range(tiles)]
    peak = parts[0]
    for part in parts[1:]:
        peak = jnp.maximum(peak, part)
    top = jnp.broadcast_to(jnp.max(peak, axis=1, keepdims=True), (rows, LANES))
    if state is not None:
        top = jnp.maximum(top, state[0])
    weights = jnp.concatenate(
        [jnp.exp2((part - top) * scale).astype(jnp.bfloat16) for part in parts], axis=1
    )
    sums = jnp.dot(weights, values, preferred_element_type=jnp.float32)
    if state is not None:
        fade = jnp.exp2((state[0] - top) * scale)
        sums = sums + state[1] * jnp.concatenate([fade, fade], axis=1)
    return top, sums


def attend_head(h, query_ref, unit_refs, state, scale):
    head_size = unit_refs[0].shape[1] // 2
    query = query_ref[:, h * head_size : (h + 1) * head_size]
    pieces = [(u, at) for u in unit_refs for at in range(0, u.shape[0], LANES)]
    step = BLOCK // LANES
    for start in range(0, len(pieces), step):
        block = pieces[start : start + step]
        keys = jnp.concatenate([u[at : at + LANES, :head_size] for u, at in block], axis=0)
        values = jnp.concatenate([u[at : at + LANES, head_size:] for u, at in block], axis=0)
        values = jnp.concatenate([values, jnp.ones_like(values)], axis=1)
        state = softmax_block(query, keys, values, state, scale)
    return state


def attend(queries, units, state):
    rows, width = queries.shape
    head_size = units[0].shape[1] // 2
    heads = width // head_size
    scale = head_size ** (-0.5) * math.log2(math.e)

    def kernel(*refs):
        query_ref, refs = refs[0], refs[1:]
        unit_refs, refs = refs[: len(units)], refs[len(units) :]
        top_out, sums_out = refs[-2:]
        for h in range(heads):
            at = slice(h * rows, (h + 1) * rows)
            before = None if state is None else (refs[0][at], refs[1][at])
            top, sums = attend_head(h, query_ref, unit_refs, before, scale)
            top_out[at] = top
            sums_out[at] = sums

    vmem = pl.BlockSpec(memory_space=pltpu.VMEM)
    args = [queries, *units, *(state or ())]
    return pl.pallas_call(
        kernel,
        out_shape=(
            pltpu.VMEM((heads * rows, LANES), jnp.float32),
            pltpu.VMEM((heads * rows, 2 * head_size), jnp.float32),
        ),
        in_specs=[vmem] * len(args),
        out_specs=(vmem, vmem),
        compiler_params=pltpu.CompilerParams(vmem_limit_bytes=16 << 20),
    )(*[in_vmem(x) for x in args])


def finish(queries, units, state, out_weight):
    rows, width = queries.shape
    head_size = units[0].shape[1] // 2
    heads = width // head_size
    scale = head_size ** (-0.5) * math.log2(math.e)
    columns = out_weight.shape[1]
    strip = math.gcd(columns, 512)
    strips = columns // strip

    def kernel(*refs):
        query_ref, refs = refs[0], refs[1:]
        unit_refs, refs = refs[: len(units)], refs[len(units) :]
        weight_ref, out_ref, attended, staged, sems = refs[-5:]
        for h in range(heads):
            at = slice(h * rows, (h + 1) * rows)
            before = None if state is None else (refs[0][at], refs[1][at])
            _, sums = attend_head(h, query_ref, unit_refs, before, scale)
            attended[:, h * head_size : (h + 1) * head_size] = (
                sums[:, :head_size] / sums[:, head_size:]
            ).astype(jnp.bfloat16)
        left = attended[...]
        copies = []
        for j in range(strips):
            at = slice(j * strip, (j + 1) * strip)
            staged[:, at] = jnp.dot(left, weight_ref[:, at], preferred_element_type=jnp.float32).astype(
                jnp.bfloat16
            )
            window = pl.ds(j * strip, strip)
            copy = pltpu.make_async_copy(staged.at[:, window], out_ref.at[:, window], sems.at[j])
            copy.start()
            copies.append(copy)
        for copy in copies:
            copy.wait()

    vmem = pl.BlockSpec(memory_space=pltpu.VMEM)
    args = [queries, *units, *(state or ()), out_weight]
    return pl.pallas_call(
        kernel,
        out_shape=jax.ShapeDtypeStruct((rows, columns), jnp.bfloat16),
        in_specs=[vmem] * len(args),
        out_specs=pl.BlockSpec(memory_space=pl.ANY),
        scratch_shapes=[
            pltpu.VMEM((rows, width), jnp.bfloat16),
            pltpu.VMEM((rows, columns), jnp.bfloat16),
            pltpu.SemaphoreType.DMA((strips,)),
        ],
        compiler_params=pltpu.CompilerParams(vmem_limit_bytes=16 << 20),
    )(*[in_vmem(x) for x in args])


def gather(own, size):
    low = 16
    if size > low:
        along = [[high * low + i for high in range(size // low)] for i in range(low)]
        own = lax.all_gather(own, "col", axis=0, tiled=True, axis_index_groups=along)
    rows = own.shape[0]
    known = {0: (0, own)}
    results = []
    for mask, held in HOPS:
        parts = []
        for m in held:
            at, array = known[m]
            parts.append(array if array.shape[0] == rows else array[at * rows : (at + 1) * rows])
        source = parts[0] if len(parts) == 1 else jnp.concatenate(parts, axis=0)
        got = lax.ppermute(source, "col", [(j, j ^ mask) for j in range(size)])
        for at, m in enumerate(held):
            known[m ^ mask] = (at, got)
        results.append(got)
    return own, results


def solution(mesh):
    size = mesh.shape["col"]

    def per_device(queries, keys, values, out_weight):
        own = jnp.concatenate([keys, values], axis=1)
        if size % 16:
            return finish(queries, [lax.all_gather(own, "col", axis=0, tiled=True)], None, out_weight)
        own, got = gather(own, size)
        units = [[own if i < 0 else got[i] for i in group] for group in GROUPS]
        state = None
        for group in units[:-1]:
            state = attend(queries, group, state)
        return finish(queries, units[-1], state, out_weight)

    spec = P(("groups", "col"), None)
    return jax.shard_map(
        per_device, mesh=mesh, in_specs=(spec, spec, spec, P()), out_specs=spec, check_vma=False
    )
```

```python
import math

import jax
import jax.numpy as jnp
from jax import lax
from jax.experimental import pallas as pl
from jax.experimental.pallas import tpu as pltpu
from jax.sharding import PartitionSpec as P

LANES = 128
BLOCK = 1024
PLAN = (
    ("hop", 8, (0,)),
    ("hop", 4, (0,)),
    ("hop", 2, (0,)),
    ("hop", 1, (0,)),
    ("attend", (0, 1), 2),
    ("hop", 4, (8,)),
    ("hop", 2, (4, 8)),
    ("hop", 1, (2, 4)),
    ("hop", 2, (12,)),
    ("hop", 1, (8, 12)),
    ("attend", (2, 3, 4, 5, 8, 9, 12, 13), 4),
    ("hop", 1, (6, 10)),
    ("hop", 1, (14,)),
)


def in_vmem(x):
    return pltpu.with_memory_space_constraint(x, pltpu.VMEM)


def in_hbm(x):
    return pltpu.with_memory_space_constraint(x, pltpu.HBM)


class Fetch:
    def __init__(self, source, begin, out, sems):
        self.half = out.shape[0] // 2
        self.source, self.begin, self.out, self.sems = source, begin, out, sems

    def copy(self, i):
        at = pl.multiple_of(i * self.half, 16)
        return pltpu.make_async_copy(
            self.source.at[pl.ds(self.begin + at, self.half)], self.out.at[pl.ds(at, self.half)], self.sems.at[i]
        )

    def start(self):
        def one(i, carry):
            self.copy(i).start()
            return carry

        lax.fori_loop(0, 2, one, 0)

    def wait(self):
        for i in range(2):
            self.copy(i).wait()


def softmax_block(query, keys, values, state, scale):
    rows = query.shape[0]
    tiles = keys.shape[0] // LANES
    scores = lax.dot_general(query, keys, (((1,), (1,)), ((), ())), preferred_element_type=jnp.float32)
    parts = [scores[:, i * LANES : (i + 1) * LANES] for i in range(tiles)]
    peak = parts[0]
    for part in parts[1:]:
        peak = jnp.maximum(peak, part)
    top = jnp.broadcast_to(jnp.max(peak, axis=1, keepdims=True), (rows, LANES))
    if state is not None:
        top = jnp.maximum(top, state[0])
    weights = jnp.concatenate(
        [jnp.exp2((part - top) * scale).astype(jnp.bfloat16) for part in parts], axis=1
    )
    sums = jnp.dot(weights, values, preferred_element_type=jnp.float32)
    if state is not None:
        fade = jnp.exp2((state[0] - top) * scale)
        sums = sums + state[1] * jnp.concatenate([fade, fade], axis=1)
    return top, sums


def attend_head(h, query_ref, unit_refs, state, scale):
    head_size = unit_refs[0].shape[1] // 2
    query = query_ref[:, h * head_size : (h + 1) * head_size]
    pieces = [(u, at) for u in unit_refs for at in range(0, u.shape[0], LANES)]
    step = BLOCK // LANES
    for start in range(0, len(pieces), step):
        block = pieces[start : start + step]
        keys = jnp.concatenate([u[at : at + LANES, :head_size] for u, at in block], axis=0)
        values = jnp.concatenate([u[at : at + LANES, head_size:] for u, at in block], axis=0)
        values = jnp.concatenate([values, jnp.ones_like(values)], axis=1)
        state = softmax_block(query, keys, values, state, scale)
    return state


def load(*arrays):
    keys, _, queries = arrays
    rows, head_size = keys.shape

    def kernel(key_ref, value_ref, query_ref, own_ref, queries_out, sems):
        copies = [
            pltpu.make_async_copy(key_ref, own_ref.at[:, pl.ds(0, head_size)], sems.at[0]),
            pltpu.make_async_copy(value_ref, own_ref.at[:, pl.ds(head_size, head_size)], sems.at[1]),
            pltpu.make_async_copy(query_ref, queries_out, sems.at[2]),
        ]
        for copy in copies:
            copy.start()
        for copy in copies:
            copy.wait()

    whole = pl.BlockSpec(memory_space=pltpu.HBM)
    vmem = pl.BlockSpec(memory_space=pltpu.VMEM)
    return pl.pallas_call(
        kernel,
        out_shape=(pltpu.VMEM((rows, 2 * head_size), keys.dtype), pltpu.VMEM(queries.shape, queries.dtype)),
        in_specs=[whole] * 3,
        out_specs=(vmem, vmem),
        scratch_shapes=[pltpu.SemaphoreType.DMA((3,))],
        compiler_params=pltpu.CompilerParams(vmem_limit_bytes=4 << 20),
    )(*[in_hbm(x) for x in arrays])


def attend(queries, units, state, out_weight, share):
    rows, width = queries.shape
    head_size = units[0].shape[1] // 2
    heads = width // head_size
    scale = head_size ** (-0.5) * math.log2(math.e)

    def kernel(*refs):
        query_ref, refs = refs[0], refs[1:]
        unit_refs, refs = refs[: len(units)], refs[len(units) :]
        weight_ref, top_out, sums_out, weight_out, sems = refs[-5:]
        fetch = Fetch(weight_ref, share[0], weight_out, sems)
        fetch.start()
        for h in range(heads):
            at = slice(h * rows, (h + 1) * rows)
            before = None if state is None else (refs[0][at], refs[1][at])
            top, sums = attend_head(h, query_ref, unit_refs, before, scale)
            top_out[at] = top
            sums_out[at] = sums
        fetch.wait()

    vmem = pl.BlockSpec(memory_space=pltpu.VMEM)
    args = [queries, *units, *(state or ())]
    *state, weight = pl.pallas_call(
        kernel,
        out_shape=(
            pltpu.VMEM((heads * rows, LANES), jnp.float32),
            pltpu.VMEM((heads * rows, 2 * head_size), jnp.float32),
            pltpu.VMEM((share[1], out_weight.shape[1]), out_weight.dtype),
        ),
        in_specs=[vmem] * len(args) + [pl.BlockSpec(memory_space=pltpu.HBM)],
        out_specs=(vmem, vmem, vmem),
        scratch_shapes=[pltpu.SemaphoreType.DMA((2,))],
        compiler_params=pltpu.CompilerParams(vmem_limit_bytes=16 << 20),
    )(*[in_vmem(x) for x in args], in_hbm(out_weight))
    return state, weight


def finish(queries, units, state, weights, out_weight):
    rows, width = queries.shape
    head_size = units[0].shape[1] // 2
    heads = width // head_size
    scale = head_size ** (-0.5) * math.log2(math.e)
    columns = out_weight.shape[1]
    begin = sum(w.shape[0] for w in weights)
    strip = math.gcd(columns, 512)
    strips = columns // strip

    def kernel(*refs):
        query_ref, refs = refs[0], refs[1:]
        unit_refs, refs = refs[: len(units)], refs[len(units) :]
        if state is not None:
            top_ref, sums_ref = refs[:2]
            refs = refs[2:]
        early, refs = refs[: len(weights)], refs[len(weights) :]
        weight_ref, out_ref, attended, staged, late, sems, late_sems = refs
        fetch = Fetch(weight_ref, begin, late, late_sems)
        fetch.start()
        for h in range(heads):
            at = slice(h * rows, (h + 1) * rows)
            before = None if state is None else (top_ref[at], sums_ref[at])
            _, sums = attend_head(h, query_ref, unit_refs, before, scale)
            attended[:, h * head_size : (h + 1) * head_size] = (
                sums[:, :head_size] / sums[:, head_size:]
            ).astype(jnp.bfloat16)
        left = attended[...]
        copies = []
        fetch.wait()
        for j in range(strips):
            at = slice(j * strip, (j + 1) * strip)
            right = jnp.concatenate([part[:, at] for part in (*early, late)], axis=0)
            staged[:, at] = jnp.dot(left, right, preferred_element_type=jnp.float32).astype(jnp.bfloat16)
            window = pl.ds(j * strip, strip)
            copy = pltpu.make_async_copy(staged.at[:, window], out_ref.at[:, window], sems.at[j])
            copy.start()
            copies.append(copy)
        for copy in copies:
            copy.wait()

    vmem = pl.BlockSpec(memory_space=pltpu.VMEM)
    whole = pl.BlockSpec(memory_space=pltpu.HBM)
    args = [queries, *units, *(state or ()), *weights]
    return pl.pallas_call(
        kernel,
        out_shape=jax.ShapeDtypeStruct((rows, columns), jnp.bfloat16),
        in_specs=[vmem] * len(args) + [whole],
        out_specs=whole,
        scratch_shapes=[
            pltpu.VMEM((rows, width), jnp.bfloat16),
            pltpu.VMEM((rows, columns), jnp.bfloat16),
            pltpu.VMEM((width - begin, columns), jnp.bfloat16),
            pltpu.SemaphoreType.DMA((strips,)),
            pltpu.SemaphoreType.DMA((2,)),
        ],
        compiler_params=pltpu.CompilerParams(vmem_limit_bytes=24 << 20),
    )(*[in_vmem(x) for x in args], in_hbm(out_weight))


def run_plan(own, queries, out_weight, size):
    low = 16
    if size > low:
        along = [[high * low + i for high in range(size // low)] for i in range(low)]
        own = lax.all_gather(own, "col", axis=0, tiled=True, axis_index_groups=along)
    rows = own.shape[0]
    known = {0: (0, own)}
    fresh = {0: own}
    heads = out_weight.shape[0] // (own.shape[1] // 2)
    state, weights, joined = None, [], None
    for kind, *what in PLAN:
        if kind == "hop":
            mask, held = what
            parts = []
            for m in held:
                at, array = known[m]
                parts.append(array if array.shape[0] == rows else array[at * rows : (at + 1) * rows])
            if len(parts) == 1:
                source = parts[0]
            else:
                if joined is not None:
                    parts, joined = lax.optimization_barrier((parts, joined))
                joined = source = jnp.concatenate(parts, axis=0)
            got = lax.ppermute(source, "col", [(j, j ^ mask) for j in range(size)])
            for at, m in enumerate(held):
                known[m ^ mask] = (at, got)
            fresh[held[0] ^ mask] = got
        else:
            units = [fresh.pop(m) for m in what[0] if m in fresh]
            count = what[1] * heads // 8 * (own.shape[1] // 2)
            begin = sum(w.shape[0] for w in weights)
            state, weight = attend(queries, units, state, out_weight, (begin, count))
            weights.append(weight)
    return finish(queries, list(fresh.values()), state, weights, out_weight)


def solution(mesh):
    size = mesh.shape["col"]

    def per_device(queries, keys, values, out_weight):
        own, queries = load(keys, values, queries)
        if size % 16:
            own = lax.all_gather(own, "col", axis=0, tiled=True)
            return finish(queries, [own], None, [], out_weight)
        return run_plan(own, queries, out_weight, size)

    spec = P(("groups", "col"), None)
    return jax.shard_map(
        per_device, mesh=mesh, in_specs=(spec, spec, spec, P()), out_specs=spec, check_vma=False
    )
```

```python
import math

import jax
import jax.numpy as jnp
from jax import lax
from jax.experimental import pallas as pl
from jax.experimental.pallas import tpu as pltpu
from jax.sharding import PartitionSpec as P

LANES = 128
BLOCK = 1024
PLAN = (
    ("hop", 8, (0,)),
    ("hop", 12, (0,)),
    ("hop", 2, (0,)),
    ("hop", 1, (0,)),
    ("hop", 4, (0,)),
    ("hop", 4, (2,)),
    ("hop", 2, (8, 12)),
    ("attend", (0, 1)),
    ("hop", 1, (2, 4, 8, 12)),
    ("attend", (2, 4, 8, 12)),
    ("hop", 1, (6, 10, 14)),
    ("attend", (3, 5, 9, 13, 6, 10, 14)),
)


def in_vmem(x):
    return pltpu.with_memory_space_constraint(x, pltpu.VMEM)


def in_hbm(x):
    return pltpu.with_memory_space_constraint(x, pltpu.HBM)


def softmax_block(query, keys, values, state, scale):
    rows = query.shape[0]
    tiles = keys.shape[0] // LANES
    scores = lax.dot_general(query, keys, (((1,), (1,)), ((), ())), preferred_element_type=jnp.float32)
    parts = [scores[:, i * LANES : (i + 1) * LANES] for i in range(tiles)]
    peak = parts[0]
    for part in parts[1:]:
        peak = jnp.maximum(peak, part)
    top = jnp.broadcast_to(jnp.max(peak, axis=1, keepdims=True), (rows, LANES))
    if state is not None:
        top = jnp.maximum(top, state[0])
    weights = jnp.concatenate(
        [jnp.exp2((part - top) * scale).astype(jnp.bfloat16) for part in parts], axis=1
    )
    sums = jnp.dot(weights, values, preferred_element_type=jnp.float32)
    if state is not None:
        fade = jnp.exp2((state[0] - top) * scale)
        sums = sums + state[1] * jnp.concatenate([fade, fade], axis=1)
    return top, sums


def attend_head(h, query_ref, unit_refs, state, scale):
    head_size = unit_refs[0].shape[1] // 2
    query = query_ref[:, h * head_size : (h + 1) * head_size]
    pieces = [(u, at) for u in unit_refs for at in range(0, u.shape[0], LANES)]
    step = BLOCK // LANES
    for start in range(0, len(pieces), step):
        block = pieces[start : start + step]
        keys = jnp.concatenate([u[at : at + LANES, :head_size] for u, at in block], axis=0)
        values = jnp.concatenate([u[at : at + LANES, head_size:] for u, at in block], axis=0)
        values = jnp.concatenate([values, jnp.ones_like(values)], axis=1)
        state = softmax_block(query, keys, values, state, scale)
    return state


def load(*arrays):
    keys, _, queries = arrays
    rows, head_size = keys.shape

    def kernel(key_ref, value_ref, query_ref, own_ref, queries_out, sems):
        copies = [
            pltpu.make_async_copy(key_ref, own_ref.at[:, pl.ds(0, head_size)], sems.at[0]),
            pltpu.make_async_copy(value_ref, own_ref.at[:, pl.ds(head_size, head_size)], sems.at[1]),
            pltpu.make_async_copy(query_ref, queries_out, sems.at[2]),
        ]
        for copy in copies:
            copy.start()
        for copy in copies:
            copy.wait()

    whole = pl.BlockSpec(memory_space=pltpu.HBM)
    vmem = pl.BlockSpec(memory_space=pltpu.VMEM)
    return pl.pallas_call(
        kernel,
        out_shape=(pltpu.VMEM((rows, 2 * head_size), keys.dtype), pltpu.VMEM(queries.shape, queries.dtype)),
        in_specs=[whole] * 3,
        out_specs=(vmem, vmem),
        scratch_shapes=[pltpu.SemaphoreType.DMA((3,))],
        compiler_params=pltpu.CompilerParams(vmem_limit_bytes=4 << 20),
    )(*[in_hbm(x) for x in arrays])


def attend(queries, units, state, last=False):
    rows, width = queries.shape
    head_size = units[0].shape[1] // 2
    heads = width // head_size
    scale = head_size ** (-0.5) * math.log2(math.e)

    def kernel(*refs):
        query_ref, refs = refs[0], refs[1:]
        unit_refs, refs = refs[: len(units)], refs[len(units) :]
        for h in range(heads):
            at = slice(h * rows, (h + 1) * rows)
            before = None if state is None else (refs[0][at], refs[1][at])
            top, sums = attend_head(h, query_ref, unit_refs, before, scale)
            if last:
                refs[-1][:, h * head_size : (h + 1) * head_size] = (
                    sums[:, :head_size] / sums[:, head_size:]
                ).astype(jnp.bfloat16)
            else:
                refs[-2][at] = top
                refs[-1][at] = sums

    vmem = pl.BlockSpec(memory_space=pltpu.VMEM)
    args = [queries, *units, *(state or ())]
    if last:
        out_shape = pltpu.VMEM((rows, width), jnp.bfloat16)
    else:
        out_shape = (
            pltpu.VMEM((heads * rows, LANES), jnp.float32),
            pltpu.VMEM((heads * rows, 2 * head_size), jnp.float32),
        )
    return pl.pallas_call(
        kernel,
        out_shape=out_shape,
        in_specs=[vmem] * len(args),
        out_specs=vmem if last else (vmem, vmem),
        compiler_params=pltpu.CompilerParams(vmem_limit_bytes=16 << 20),
    )(*[in_vmem(x) for x in args])


def project(attended, out_weight):
    return jnp.dot(attended, out_weight, preferred_element_type=jnp.float32).astype(jnp.bfloat16)


def run_plan(own, queries, size):
    low = 16
    if size > low:
        along = [[high * low + i for high in range(size // low)] for i in range(low)]
        own = lax.all_gather(own, "col", axis=0, tiled=True, axis_index_groups=along)
    rows = own.shape[0]
    known = {0: (0, own)}
    fresh = {0: own}
    state, joined = None, None
    for kind, *what in PLAN:
        if kind == "hop":
            mask, held = what
            parts = []
            for m in held:
                at, array = known[m]
                parts.append(array if array.shape[0] == rows else array[at * rows : (at + 1) * rows])
            if len(parts) == 1:
                source = parts[0]
            else:
                if joined is not None:
                    parts, joined = lax.optimization_barrier((parts, joined))
                joined = source = jnp.concatenate(parts, axis=0)
            got = lax.ppermute(source, "col", [(j, j ^ mask) for j in range(size)])
            for at, m in enumerate(held):
                known[m ^ mask] = (at, got)
            fresh[held[0] ^ mask] = got
        else:
            units = [fresh.pop(m) for m in what[0] if m in fresh]
            state = attend(queries, units, state)
    return attend(queries, list(fresh.values()), state, True)


def solution(mesh):
    size = mesh.shape["col"]

    def per_device(queries, keys, values, out_weight):
        own, queries = load(keys, values, queries)
        if size % 16:
            own = lax.all_gather(own, "col", axis=0, tiled=True)
            return project(attend(queries, [own], None, True), out_weight)
        return project(run_plan(own, queries, size), out_weight)

    spec = P(("groups", "col"), None)
    return jax.shard_map(
        per_device, mesh=mesh, in_specs=(spec, spec, spec, P()), out_specs=spec, check_vma=False
    )
```

```python
import math

import jax
import jax.numpy as jnp
from jax import lax
from jax.experimental import pallas as pl
from jax.experimental.pallas import tpu as pltpu
from jax.sharding import PartitionSpec as P

LANES = 128
BLOCK = 1024
PLAN = (
    ("hop", 8, (0,)),
    ("hop", 12, (0,)),
    ("hop", 2, (0,)),
    ("hop", 1, (0,)),
    ("hop", 4, (0,)),
    ("load", ()),
    ("hop", 4, (2,)),
    ("hop", 2, (8, 12)),
    ("attend", (0, 1)),
    ("hop", 1, (2, 4, 8)),
    ("attend", (2, 4, 8, 12)),
    ("hop", 1, (12, 6)),
    ("attend", (3, 5, 9)),
    ("hop", 1, (10, 14)),
    ("attend", (6, 10, 14, 7, 13)),
)


def in_vmem(x):
    return pltpu.with_memory_space_constraint(x, pltpu.VMEM)


def in_hbm(x):
    return pltpu.with_memory_space_constraint(x, pltpu.HBM)


def softmax_block(query, keys, values, state, scale):
    rows = query.shape[0]
    tiles = keys.shape[0] // LANES
    scores = lax.dot_general(query, keys, (((1,), (1,)), ((), ())), preferred_element_type=jnp.float32)
    parts = [scores[:, i * LANES : (i + 1) * LANES] for i in range(tiles)]
    peak = parts[0]
    for part in parts[1:]:
        peak = jnp.maximum(peak, part)
    top = jnp.broadcast_to(jnp.max(peak, axis=1, keepdims=True), (rows, LANES))
    if state is not None:
        top = jnp.maximum(top, state[0])
    weights = jnp.concatenate(
        [jnp.exp2((part - top) * scale).astype(jnp.bfloat16) for part in parts], axis=1
    )
    sums = jnp.dot(weights, values, preferred_element_type=jnp.float32)
    if state is not None:
        fade = jnp.exp2((state[0] - top) * scale)
        sums = sums + state[1] * jnp.concatenate([fade, fade], axis=1)
    return top, sums


def attend_head(h, query_ref, unit_refs, state, scale):
    head_size = unit_refs[0].shape[1] // 2
    query = query_ref[:, h * head_size : (h + 1) * head_size]
    pieces = [(u, at) for u in unit_refs for at in range(0, u.shape[0], LANES)]
    step = BLOCK // LANES
    for start in range(0, len(pieces), step):
        block = pieces[start : start + step]
        keys = jnp.concatenate([u[at : at + LANES, :head_size] for u, at in block], axis=0)
        values = jnp.concatenate([u[at : at + LANES, head_size:] for u, at in block], axis=0)
        values = jnp.concatenate([values, jnp.ones_like(values)], axis=1)
        state = softmax_block(query, keys, values, state, scale)
    return state


def load(*arrays):
    rows = arrays[0].shape[0]
    width = sum(x.shape[1] for x in arrays)

    def kernel(*refs):
        *sources, out_ref, sems = refs
        copies = []
        at = 0
        for i, source in enumerate(sources):
            window = out_ref.at[:, pl.ds(at, source.shape[1])] if len(sources) > 1 else out_ref
            copies.append(pltpu.make_async_copy(source, window, sems.at[i]))
            at += source.shape[1]
        for copy in copies:
            copy.start()
        for copy in copies:
            copy.wait()

    return pl.pallas_call(
        kernel,
        out_shape=pltpu.VMEM((rows, width), arrays[0].dtype),
        in_specs=[pl.BlockSpec(memory_space=pltpu.HBM)] * len(arrays),
        out_specs=pl.BlockSpec(memory_space=pltpu.VMEM),
        scratch_shapes=[pltpu.SemaphoreType.DMA((len(arrays),))],
        compiler_params=pltpu.CompilerParams(vmem_limit_bytes=4 << 20),
    )(*[in_hbm(x) for x in arrays])


def attend(queries, units, state, last=False):
    rows, width = queries.shape
    head_size = units[0].shape[1] // 2
    heads = width // head_size
    scale = head_size ** (-0.5) * math.log2(math.e)

    def kernel(*refs):
        query_ref, refs = refs[0], refs[1:]
        unit_refs, refs = refs[: len(units)], refs[len(units) :]
        for h in range(heads):
            at = slice(h * rows, (h + 1) * rows)
            before = None if state is None else (refs[0][at], refs[1][at])
            top, sums = attend_head(h, query_ref, unit_refs, before, scale)
            if last:
                refs[-1][:, h * head_size : (h + 1) * head_size] = (
                    sums[:, :head_size] / sums[:, head_size:]
                ).astype(jnp.bfloat16)
            else:
                refs[-2][at] = top
                refs[-1][at] = sums

    vmem = pl.BlockSpec(memory_space=pltpu.VMEM)
    args = [queries, *units, *(state or ())]
    if last:
        out_shape = pltpu.VMEM((rows, width), jnp.bfloat16)
    else:
        out_shape = (
            pltpu.VMEM((heads * rows, LANES), jnp.float32),
            pltpu.VMEM((heads * rows, 2 * head_size), jnp.float32),
        )
    return pl.pallas_call(
        kernel,
        out_shape=out_shape,
        in_specs=[vmem] * len(args),
        out_specs=vmem if last else (vmem, vmem),
        compiler_params=pltpu.CompilerParams(vmem_limit_bytes=16 << 20),
    )(*[in_vmem(x) for x in args])


def project(attended, out_weight):
    return jnp.dot(attended, out_weight, preferred_element_type=jnp.float32).astype(jnp.bfloat16)


def run_plan(own, queries, size):
    low = 16
    if size > low:
        along = [[high * low + i for high in range(size // low)] for i in range(low)]
        own = lax.all_gather(own, "col", axis=0, tiled=True, axis_index_groups=along)
    rows = own.shape[0]
    known = {0: (0, own)}
    fresh = {0: own}
    state, joined = None, None
    for kind, *what in PLAN:
        if kind == "hop":
            mask, held = what
            parts = []
            for m in held:
                at, array = known[m]
                parts.append(array if array.shape[0] == rows else array[at * rows : (at + 1) * rows])
            arrays = [known[m][1] for m in held]
            if len(parts) == 1:
                source = parts[0]
            elif [known[m][0] for m in held] == list(range(arrays[0].shape[0] // rows)) and all(
                array is arrays[0] for array in arrays
            ):
                source = arrays[0]
            else:
                if joined is not None:
                    parts, joined = lax.optimization_barrier((parts, joined))
                joined = source = jnp.concatenate(parts, axis=0)
            got = lax.ppermute(source, "col", [(j, j ^ mask) for j in range(size)])
            for at, m in enumerate(held):
                known[m ^ mask] = (at, got)
            fresh[held[0] ^ mask] = got
        elif kind == "load":
            queries = load(queries)
        else:
            units = [fresh.pop(m) for m in what[0] if m in fresh]
            state = attend(queries, units, state)
    return attend(queries, list(fresh.values()), state, True)


def solution(mesh):
    size = mesh.shape["col"]

    def per_device(queries, keys, values, out_weight):
        own = load(keys, values)
        if size % 16:
            own = lax.all_gather(own, "col", axis=0, tiled=True)
            return project(attend(load(queries), [own], None, True), out_weight)
        return project(run_plan(own, queries, size), out_weight)

    spec = P(("groups", "col"), None)
    return jax.shard_map(
        per_device, mesh=mesh, in_specs=(spec, spec, spec, P()), out_specs=spec, check_vma=False
    )
```

```python
import math

import jax
import jax.numpy as jnp
from jax import lax
from jax.experimental import pallas as pl
from jax.experimental.pallas import tpu as pltpu
from jax.sharding import PartitionSpec as P

LANES = 128
BLOCK = 1024
PLAN = (
    ("hop", 8, (0,)),
    ("hop", 12, (0,)),
    ("hop", 2, (0,)),
    ("hop", 1, (0,)),
    ("hop", 4, (0,)),
    ("hop", 4, (2,)),
    ("hop", 2, (8, 12)),
    ("hop", 1, (2, 4, 8, 12)),
    ("attend", (0, 1, 2, 4, 8, 12)),
    ("hop", 1, (6,)),
    ("attend", (3, 5, 9, 13)),
    ("hop", 1, (10, 14)),
    ("attend", (6, 10, 14, 7)),
)


def in_vmem(x):
    return pltpu.with_memory_space_constraint(x, pltpu.VMEM)


def in_hbm(x):
    return pltpu.with_memory_space_constraint(x, pltpu.HBM)


def softmax_block(query, keys, values, state, scale):
    rows = query.shape[0]
    tiles = keys.shape[0] // LANES
    scores = lax.dot_general(query, keys, (((1,), (1,)), ((), ())), preferred_element_type=jnp.float32)
    parts = [scores[:, i * LANES : (i + 1) * LANES] for i in range(tiles)]
    peak = parts[0]
    for part in parts[1:]:
        peak = jnp.maximum(peak, part)
    top = jnp.broadcast_to(jnp.max(peak, axis=1, keepdims=True), (rows, LANES))
    if state is not None:
        top = jnp.maximum(top, state[0])
    weights = jnp.concatenate(
        [jnp.exp2((part - top) * scale).astype(jnp.bfloat16) for part in parts], axis=1
    )
    sums = jnp.dot(weights, values, preferred_element_type=jnp.float32)
    if state is not None:
        fade = jnp.exp2((state[0] - top) * scale)
        sums = sums + state[1] * jnp.concatenate([fade, fade], axis=1)
    return top, sums


def attend_head(h, query_ref, unit_refs, state, scale):
    head_size = unit_refs[0].shape[1] // 2
    query = query_ref[:, h * head_size : (h + 1) * head_size]
    pieces = [(u, at) for u in unit_refs for at in range(0, u.shape[0], LANES)]
    step = BLOCK // LANES
    for start in range(0, len(pieces), step):
        block = pieces[start : start + step]
        keys = jnp.concatenate([u[at : at + LANES, :head_size] for u, at in block], axis=0)
        values = jnp.concatenate([u[at : at + LANES, head_size:] for u, at in block], axis=0)
        values = jnp.concatenate([values, jnp.ones_like(values)], axis=1)
        state = softmax_block(query, keys, values, state, scale)
    return state


def load(*arrays):
    keys, _, queries = arrays
    rows, head_size = keys.shape
    pieces = math.gcd(rows // 16, 8)

    def kernel(key_ref, value_ref, query_ref, own_ref, queries_out, sems):
        copies = [
            pltpu.make_async_copy(key_ref, own_ref.at[:, pl.ds(0, head_size)], sems.at[0]),
            pltpu.make_async_copy(value_ref, own_ref.at[:, pl.ds(head_size, head_size)], sems.at[1]),
        ]
        for i in range(pieces):
            at = pl.ds(i * (rows // pieces), rows // pieces)
            copies.append(pltpu.make_async_copy(query_ref.at[at], queries_out.at[at], sems.at[2 + i]))
        for copy in copies:
            copy.start()
        for copy in copies:
            copy.wait()

    whole = pl.BlockSpec(memory_space=pltpu.HBM)
    vmem = pl.BlockSpec(memory_space=pltpu.VMEM)
    return pl.pallas_call(
        kernel,
        out_shape=(pltpu.VMEM((rows, 2 * head_size), keys.dtype), pltpu.VMEM(queries.shape, queries.dtype)),
        in_specs=[whole] * 3,
        out_specs=(vmem, vmem),
        scratch_shapes=[pltpu.SemaphoreType.DMA((2 + pieces,))],
        compiler_params=pltpu.CompilerParams(vmem_limit_bytes=4 << 20),
    )(*[in_hbm(x) for x in arrays])


def attend(queries, units, state, last=False):
    rows, width = queries.shape
    head_size = units[0].shape[1] // 2
    heads = width // head_size
    scale = head_size ** (-0.5) * math.log2(math.e)

    def kernel(*refs):
        query_ref, refs = refs[0], refs[1:]
        unit_refs, refs = refs[: len(units)], refs[len(units) :]
        for h in range(heads):
            at = slice(h * rows, (h + 1) * rows)
            before = None if state is None else (refs[0][at], refs[1][at])
            top, sums = attend_head(h, query_ref, unit_refs, before, scale)
            if last:
                refs[-1][:, h * head_size : (h + 1) * head_size] = (
                    sums[:, :head_size] / sums[:, head_size:]
                ).astype(jnp.bfloat16)
            else:
                refs[-2][at] = top
                refs[-1][at] = sums

    vmem = pl.BlockSpec(memory_space=pltpu.VMEM)
    args = [queries, *units, *(state or ())]
    if last:
        out_shape = pltpu.VMEM((rows, width), jnp.bfloat16)
    else:
        out_shape = (
            pltpu.VMEM((heads * rows, LANES), jnp.float32),
            pltpu.VMEM((heads * rows, 2 * head_size), jnp.float32),
        )
    return pl.pallas_call(
        kernel,
        out_shape=out_shape,
        in_specs=[vmem] * len(args),
        out_specs=vmem if last else (vmem, vmem),
        compiler_params=pltpu.CompilerParams(vmem_limit_bytes=16 << 20),
    )(*[in_vmem(x) for x in args])


def project(attended, out_weight):
    return jnp.dot(attended, out_weight, preferred_element_type=jnp.float32).astype(jnp.bfloat16)


def run_plan(own, queries, size):
    low = 16
    if size > low:
        along = [[high * low + i for high in range(size // low)] for i in range(low)]
        own = lax.all_gather(own, "col", axis=0, tiled=True, axis_index_groups=along)
    rows = own.shape[0]
    known = {0: (0, own)}
    fresh = {0: own}
    state, joined = None, None
    for kind, *what in PLAN:
        if kind == "hop":
            mask, held = what
            parts = []
            for m in held:
                at, array = known[m]
                parts.append(array if array.shape[0] == rows else array[at * rows : (at + 1) * rows])
            arrays = [known[m][1] for m in held]
            if len(parts) == 1:
                source = parts[0]
            elif [known[m][0] for m in held] == list(range(arrays[0].shape[0] // rows)) and all(
                array is arrays[0] for array in arrays
            ):
                source = arrays[0]
            else:
                if joined is not None:
                    parts, joined = lax.optimization_barrier((parts, joined))
                joined = source = jnp.concatenate(parts, axis=0)
            got = lax.ppermute(source, "col", [(j, j ^ mask) for j in range(size)])
            for at, m in enumerate(held):
                known[m ^ mask] = (at, got)
            fresh[held[0] ^ mask] = got
        else:
            units = [fresh.pop(m) for m in what[0] if m in fresh]
            state = attend(queries, units, state)
    return attend(queries, list(fresh.values()), state, True)


def solution(mesh):
    size = mesh.shape["col"]

    def per_device(queries, keys, values, out_weight):
        own, queries = load(keys, values, queries)
        if size % 16:
            own = lax.all_gather(own, "col", axis=0, tiled=True)
            return project(attend(queries, [own], None, True), out_weight)
        return project(run_plan(own, queries, size), out_weight)

    spec = P(("groups", "col"), None)
    return jax.shard_map(
        per_device, mesh=mesh, in_specs=(spec, spec, spec, P()), out_specs=spec, check_vma=False
    )
```

```python
import math

import jax
import jax.numpy as jnp
from jax import lax
from jax.experimental import pallas as pl
from jax.experimental.pallas import tpu as pltpu
from jax.sharding import PartitionSpec as P

LANES = 128
BLOCK = 1024
PLAN = (
    ("hop", 8, (0,)),
    ("hop", 12, (0,)),
    ("hop", 2, (0,)),
    ("hop", 1, (0,)),
    ("hop", 4, (0,)),
    ("load", ()),
    ("hop", 4, (2,)),
    ("hop", 2, (8, 12)),
    ("hop", 1, (2, 4, 8, 12)),
    ("attend", (0, 1, 2, 4, 8, 12)),
    ("hop", 1, (6,)),
    ("attend", (3, 5, 9, 13)),
    ("hop", 1, (10, 14)),
    ("attend", (6, 10, 14, 7)),
)


def in_vmem(x):
    return pltpu.with_memory_space_constraint(x, pltpu.VMEM)


def in_hbm(x):
    return pltpu.with_memory_space_constraint(x, pltpu.HBM)


def softmax_block(query, keys, values, state, scale):
    rows = query.shape[0]
    tiles = keys.shape[0] // LANES
    scores = lax.dot_general(query, keys, (((1,), (1,)), ((), ())), preferred_element_type=jnp.float32)
    parts = [scores[:, i * LANES : (i + 1) * LANES] for i in range(tiles)]
    peak = parts[0]
    for part in parts[1:]:
        peak = jnp.maximum(peak, part)
    top = jnp.broadcast_to(jnp.max(peak, axis=1, keepdims=True), (rows, LANES))
    if state is not None:
        top = jnp.maximum(top, state[0])
    weights = jnp.concatenate(
        [jnp.exp2((part - top) * scale).astype(jnp.bfloat16) for part in parts], axis=1
    )
    sums = jnp.dot(weights, values, preferred_element_type=jnp.float32)
    if state is not None:
        fade = jnp.exp2((state[0] - top) * scale)
        sums = sums + state[1] * jnp.concatenate([fade, fade], axis=1)
    return top, sums


def attend_head(h, query_ref, unit_refs, state, scale):
    head_size = unit_refs[0].shape[1] // 2
    query = query_ref[:, h * head_size : (h + 1) * head_size]
    pieces = [(u, at) for u in unit_refs for at in range(0, u.shape[0], LANES)]
    step = BLOCK // LANES
    for start in range(0, len(pieces), step):
        block = pieces[start : start + step]
        keys = jnp.concatenate([u[at : at + LANES, :head_size] for u, at in block], axis=0)
        values = jnp.concatenate([u[at : at + LANES, head_size:] for u, at in block], axis=0)
        values = jnp.concatenate([values, jnp.ones_like(values)], axis=1)
        state = softmax_block(query, keys, values, state, scale)
    return state


def load(*arrays):
    rows = arrays[0].shape[0]
    width = sum(x.shape[1] for x in arrays)

    def kernel(*refs):
        *sources, out_ref, sems = refs
        copies = []
        at = 0
        for i, source in enumerate(sources):
            window = out_ref.at[:, pl.ds(at, source.shape[1])] if len(sources) > 1 else out_ref
            copies.append(pltpu.make_async_copy(source, window, sems.at[i]))
            at += source.shape[1]
        for copy in copies:
            copy.start()
        for copy in copies:
            copy.wait()

    return pl.pallas_call(
        kernel,
        out_shape=pltpu.VMEM((rows, width), arrays[0].dtype),
        in_specs=[pl.BlockSpec(memory_space=pltpu.HBM)] * len(arrays),
        out_specs=pl.BlockSpec(memory_space=pltpu.VMEM),
        scratch_shapes=[pltpu.SemaphoreType.DMA((len(arrays),))],
        compiler_params=pltpu.CompilerParams(vmem_limit_bytes=4 << 20),
    )(*[in_hbm(x) for x in arrays])


def attend(queries, units, state, last=False):
    rows, width = queries.shape
    head_size = units[0].shape[1] // 2
    heads = width // head_size
    scale = head_size ** (-0.5) * math.log2(math.e)

    def kernel(*refs):
        query_ref, refs = refs[0], refs[1:]
        unit_refs, refs = refs[: len(units)], refs[len(units) :]
        for h in range(heads):
            at = slice(h * rows, (h + 1) * rows)
            before = None if state is None else (refs[0][at], refs[1][at])
            top, sums = attend_head(h, query_ref, unit_refs, before, scale)
            if last:
                refs[-1][:, h * head_size : (h + 1) * head_size] = (
                    sums[:, :head_size] / sums[:, head_size:]
                ).astype(jnp.bfloat16)
            else:
                refs[-2][at] = top
                refs[-1][at] = sums

    vmem = pl.BlockSpec(memory_space=pltpu.VMEM)
    args = [queries, *units, *(state or ())]
    if last:
        out_shape = pltpu.VMEM((rows, width), jnp.bfloat16)
    else:
        out_shape = (
            pltpu.VMEM((heads * rows, LANES), jnp.float32),
            pltpu.VMEM((heads * rows, 2 * head_size), jnp.float32),
        )
    return pl.pallas_call(
        kernel,
        out_shape=out_shape,
        in_specs=[vmem] * len(args),
        out_specs=vmem if last else (vmem, vmem),
        compiler_params=pltpu.CompilerParams(vmem_limit_bytes=16 << 20),
    )(*[in_vmem(x) for x in args])


def project(attended, out_weight):
    return jnp.dot(attended, out_weight, preferred_element_type=jnp.float32).astype(jnp.bfloat16)


def run_plan(own, queries, size):
    low = 16
    if size > low:
        along = [[high * low + i for high in range(size // low)] for i in range(low)]
        own = lax.all_gather(own, "col", axis=0, tiled=True, axis_index_groups=along)
    rows = own.shape[0]
    known = {0: (0, own)}
    fresh = {0: own}
    state, joined = None, None
    for kind, *what in PLAN:
        if kind == "hop":
            mask, held = what
            parts = []
            for m in held:
                at, array = known[m]
                parts.append(array if array.shape[0] == rows else array[at * rows : (at + 1) * rows])
            arrays = [known[m][1] for m in held]
            if len(parts) == 1:
                source = parts[0]
            elif [known[m][0] for m in held] == list(range(arrays[0].shape[0] // rows)) and all(
                array is arrays[0] for array in arrays
            ):
                source = arrays[0]
            else:
                if joined is not None:
                    parts, joined = lax.optimization_barrier((parts, joined))
                joined = source = jnp.concatenate(parts, axis=0)
            got = lax.ppermute(source, "col", [(j, j ^ mask) for j in range(size)])
            for at, m in enumerate(held):
                known[m ^ mask] = (at, got)
            fresh[held[0] ^ mask] = got
        elif kind == "load":
            queries = load(queries)
        else:
            units = [fresh.pop(m) for m in what[0] if m in fresh]
            state = attend(queries, units, state)
    return attend(queries, list(fresh.values()), state, True)


def solution(mesh):
    size = mesh.shape["col"]

    def per_device(queries, keys, values, out_weight):
        own = load(keys, values)
        if size % 16:
            own = lax.all_gather(own, "col", axis=0, tiled=True)
            return project(attend(load(queries), [own], None, True), out_weight)
        return project(run_plan(own, queries, size), out_weight)

    spec = P(("groups", "col"), None)
    return jax.shard_map(
        per_device, mesh=mesh, in_specs=(spec, spec, spec, P()), out_specs=spec, check_vma=False
    )
```
